32 devices in a mesh: sec: 4 (over y, x), strip: 8 (over z, core).
Axes of the slice: x: 2, y: 2, z: 4, core: 2. Of those that a mesh axis runs over, the one named last changes fastest.
Arguments:
- activations: bfloat16 [2, 4, 1, 2, 1, 256, 64, 512], P(None, 'sec', None, None, None, 'strip'), may hold values from 0 to 2
- relu_masks: int32 [2, 4, 1, 2, 1, 256, 64, 512], P(None, 'sec', None, None, None, 'strip'), may hold values 0 or 1
- grad_in: bfloat16 [2, 2, 1, 256, 64, 512], P(None, None, None, 'strip'), may hold values from -6 to 6
- mix_weight: bfloat16 [4, 1, 512, 512], P('sec'), may hold values from -0.375 to 0.375
- depth_kernel: bfloat16 [4, 1, 25, 512], P('sec'), may hold values from -1.25 to 1.25
Outputs:
- segment_grads: bfloat16 [2, 4, 2, 1, 256, 64, 512], P(None, 'sec', None, None, 'strip')
- mix_grad: float32 [4, 1, 512, 512], P('sec', None, 'strip')
- kernel_grad: float32 [4, 1, 25, 512], P('sec')
The draws below stay inside these ranges and needn't reach their ends.
All inputs are finite; a program needn't handle non-finite values. No bound on the sum of `relu_masks` on one device may be relied on, other than what follows from the above.
Results may differ from the reference program's by a relative error of at most 0.025.
Values may be sent and summed in bfloat16 or wider, within the bound.
A program may use at most 192 MiB of HBM per device.

```python
import jax
import jax.numpy as jnp
from jax import lax

C = 512
H = 256
W = 64
LAYERS = 1
MICRO = 2
IMAGES = 1
SECTIONS = 4


def plant(array, rng, least, largest):
    longest = array.shape.index(max(array.shape))
    spots = []
    for shift in (0, 1):
        where = [jax.random.randint(jax.random.fold_in(rng, axis), (), 0, length) for axis, length in enumerate(array.shape)]
        where[longest] = (where[longest] + shift) % array.shape[longest]
        spots.append(tuple(where))
    return array.at[spots[0]].set(least).at[spots[1]].set(largest)


def levels(rng, extent, cuts, smallest, high):
    loudness = 1.0
    for axis_at, blocks in cuts:
        heights = jax.random.uniform(jax.random.fold_in(jax.random.fold_in(rng, 6), axis_at), (blocks,), jnp.float32, smallest / len(cuts), high / len(cuts))
        loudness = loudness * jnp.repeat(jnp.exp(heights), extent[axis_at] // blocks).reshape((-1,) + (1,) * (len(extent) - 1 - axis_at))
    return loudness


def normal_values(key, extent, spread, bound, split=(), dtype=jnp.bfloat16):
    entries = spread * jax.random.normal(key, extent, jnp.float32)
    if split:
        entries = entries * levels(key, extent, split, -0.22, 0.18)
    return jnp.clip(entries, -bound, bound).astype(dtype)


def setup_inputs(seed: int = 0) -> dict:
    key_of = jax.random.split(jax.random.key(seed), 6)
    activations = jnp.clip(2.0 * jax.random.uniform(key_of[0], (2, SECTIONS, LAYERS, MICRO, IMAGES, H, W, C), jnp.float32) ** levels(key_of[0], (2, SECTIONS, LAYERS, MICRO, IMAGES, H, W, C), ((1, 4), (5, 8)), -0.2, 0.2), 0.0, 2.0).astype(jnp.bfloat16)
    relu_masks = plant((jax.random.randint(key_of[1], (2, SECTIONS, LAYERS, MICRO, IMAGES, H, W, C), 0, 2) < 1).astype(jnp.int32), jax.random.fold_in(key_of[1], 1), 0, 1)
    grad_in = normal_values(key_of[2], (2, MICRO, IMAGES, H, W, C), 1.0, 6.0, ((3, 8),))
    mix_weight = normal_values(key_of[3], (SECTIONS, LAYERS, C, C), (C // 2) ** -0.5, 0.375, ((0, 4),))
    depth_kernel = normal_values(key_of[4], (SECTIONS, LAYERS, 25, C), 25 ** -0.5, 1.25, ((0, 4),))
    return {"activations": activations, "relu_masks": relu_masks, "grad_in": grad_in, "mix_weight": mix_weight, "depth_kernel": depth_kernel}


def forward_depth(layer_input, kernel):
    framed = jnp.pad(layer_input.astype(jnp.float32), ((0, 0), (2, 2), (2, 2), (0, 0)))
    rows, cols = layer_input.shape[1], layer_input.shape[2]
    total = jnp.zeros(layer_input.shape, jnp.float32)
    for row_tap in range(5):
        for col_tap in range(5):
            window = framed[:, row_tap:row_tap + rows, col_tap:col_tap + cols, :]
            total = total + window * kernel[row_tap * 5 + col_tap].astype(jnp.float32)
    return total, framed


def transposed_depth(back_mix, kernel):
    framed = jnp.pad(back_mix.astype(jnp.float32), ((0, 0), (2, 2), (2, 2), (0, 0)))
    rows, cols = back_mix.shape[1], back_mix.shape[2]
    total = jnp.zeros(back_mix.shape, jnp.float32)
    for row_tap in range(5):
        for col_tap in range(5):
            window = framed[:, 4 - row_tap:4 - row_tap + rows, 4 - col_tap:4 - col_tap + cols, :]
            total = total + window * kernel[row_tap * 5 + col_tap].astype(jnp.float32)
    return total


def kernel_corr(back_mix, framed):
    rows, cols = back_mix.shape[1], back_mix.shape[2]
    wide = back_mix.astype(jnp.float32)
    terms = []
    for row_tap in range(5):
        for col_tap in range(5):
            window = framed[:, row_tap:row_tap + rows, col_tap:col_tap + cols, :]
            terms.append(jnp.sum(wide * window, axis=(0, 1, 2)))
    return jnp.stack(terms)


def section_back(upstream, layer_inputs, layer_masks, weight, kernel):
    channels = upstream.shape[-1]
    weight_terms = []
    kernel_terms = []
    for layer in reversed(range(layer_inputs.shape[0])):
        depth, framed = forward_depth(layer_inputs[layer], kernel[layer])
        depth = depth.astype(jnp.bfloat16)
        gated = jnp.where(layer_masks[layer] == 1, upstream, jnp.zeros_like(upstream))
        flat_gated = gated.reshape(-1, channels)
        back_mix = jnp.dot(flat_gated, weight[layer].T, preferred_element_type=jnp.float32)
        back_mix = back_mix.astype(jnp.bfloat16).reshape(upstream.shape)
        weight_terms.insert(0, jnp.dot(depth.reshape(-1, channels).T, flat_gated, preferred_element_type=jnp.float32))
        kernel_terms.insert(0, kernel_corr(back_mix, framed))
        upstream = transposed_depth(back_mix, kernel[layer]).astype(jnp.bfloat16)
    return upstream, jnp.stack(weight_terms), jnp.stack(kernel_terms)


def reference(activations, relu_masks, grad_in, mix_weight, depth_kernel):
    weight_sums = jnp.zeros(mix_weight.shape, jnp.float32)
    kernel_sums = jnp.zeros(depth_kernel.shape, jnp.float32)
    replicas = []
    for replica in range(2):
        if replica == 0:
            weights, kernels = mix_weight, depth_kernel
        else:
            weights, kernels = jnp.flip(mix_weight, 0), jnp.flip(depth_kernel, 0)
        per_micro = []
        for micro in range(MICRO):
            def segment(upstream, inputs):
                layer_inputs, layer_masks, weight, kernel = inputs
                result, weight_term, kernel_term = section_back(upstream, layer_inputs, layer_masks, weight, kernel)
                return result, (result, weight_term, kernel_term)

            carried, (results, weight_terms, kernel_terms) = lax.scan(
                segment, grad_in[replica, micro],
                (activations[replica, :, :, micro], relu_masks[replica, :, :, micro], weights, kernels),
                reverse=(replica == 0))
            if replica == 1:
                weight_terms = jnp.flip(weight_terms, 0)
                kernel_terms = jnp.flip(kernel_terms, 0)
            weight_sums = weight_sums + weight_terms
            kernel_sums = kernel_sums + kernel_terms
            per_micro.append(results)
        replicas.append(jnp.stack(per_micro, axis=1))
    return jnp.stack(replicas), weight_sums * (1.0 / H), kernel_sums * (1.0 / H)
```

```python
import functools

import jax
import jax.numpy as jnp
import numpy as np
from jax import lax
from jax.experimental import pallas as pl
from jax.experimental.pallas import tpu as pltpu
from jax.sharding import PartitionSpec as P

H = 256
LANES = 128
CT = jnp.bfloat16
TILE = 16
ANY = pl.BlockSpec(memory_space=pl.ANY)
SMEM = pl.BlockSpec(memory_space=pltpu.SMEM)


def lane_block(block):
    return pl.ds(pl.multiple_of(block * LANES, LANES), LANES)


def shifted(value, offset, column):
    if offset == 0:
        return value
    cols = value.shape[0]
    turned = pltpu.roll(value, (-offset) % cols, 0)
    inside = column < cols - offset if offset > 0 else column >= -offset
    return jnp.where(inside, turned, 0.0)


def row_conv(source, row, lanes, taps, cols, column, sign):
    total = [None] * 5
    for row_tap in range(5):
        place = row + (row_tap if sign == 1 else 4 - row_tap)
        line = source[place, :, lanes].astype(CT).reshape(cols // TILE, TILE, LANES)
        for col_tap in range(5):
            term = line * taps[row_tap * 5 + col_tap, :, lanes][None]
            total[col_tap] = term if total[col_tap] is None else total[col_tap] + term
    out = None
    for col_tap in range(5):
        part = total[col_tap].reshape(cols, LANES).astype(jnp.float32)
        part = shifted(part, sign * (col_tap - 2), column)
        out = part if out is None else out + part
    return out


def spread_kernel(kern_ref, taps):
    channels = kern_ref.shape[1]
    for tap in range(25):
        taps[tap] = jnp.broadcast_to(kern_ref[tap : tap + 1, :].astype(CT), (TILE, channels))


def chain_kernel(replica, rows, cols, fresh, *refs):
    meta, recv, recv_top, recv_bot, entry, entry_top, entry_bot, masks, mask_top, mask_bot, weight, kern = refs[:12]
    refs = refs[12 if fresh else 15 :]
    sent, sent_top, sent_bot, outs, mixed, gates = refs[:6]
    up, seen, seen_halo, wbuf, kbuf, taps, bm, out, sems = refs[6:]
    channels = up.shape[2]
    micro = meta[1]

    @pl.when(meta[0] == 1)
    def _():
        loads = [
            pltpu.make_async_copy(masks.at[replica, 0, 0, micro, 0], seen, sems.at[0]),
            pltpu.make_async_copy(mask_top.at[replica, micro], seen_halo.at[pl.ds(0, 2)], sems.at[1]),
            pltpu.make_async_copy(mask_bot.at[replica, micro], seen_halo.at[pl.ds(2, 2)], sems.at[2]),
            pltpu.make_async_copy(weight.at[replica], wbuf, sems.at[3]),
            pltpu.make_async_copy(kern.at[replica], kbuf, sems.at[4]),
        ]
        for load in loads:
            load.start()

        def fetch(main, top, bot):
            pieces = [
                pltpu.make_async_copy(main, up.at[pl.ds(2, rows)], sems.at[5]),
                pltpu.make_async_copy(top, up.at[pl.ds(0, 2)], sems.at[6]),
                pltpu.make_async_copy(bot, up.at[pl.ds(rows + 2, 2)], sems.at[7]),
            ]
            for piece in pieces:
                piece.start()
            for piece in pieces:
                piece.wait()

        @pl.when(meta[2] == 1)
        def _():
            fetch(entry.at[replica, micro, 0], entry_top.at[replica, micro], entry_bot.at[replica, micro])

        @pl.when(meta[2] == 0)
        def _():
            fetch(recv, recv_top, recv_bot)

        for load in loads:
            load.wait()
        spread_kernel(kbuf, taps)
        for line in range(2):
            up[line] = up[line] * seen_halo[line]
            up[rows + 2 + line] = up[rows + 2 + line] * seen_halo[2 + line]

        @pl.loop(0, rows)
        def _(row):
            value = up[row + 2].astype(jnp.float32)
            up[row + 2] = jnp.where(seen[row] == 1, value, 0.0).astype(jnp.bfloat16)

        save_gates = pltpu.make_async_copy(up.at[pl.ds(2, rows)], gates.at[replica, micro], sems.at[0])
        save_gates.start()

        @pl.loop(0, (rows + 4) // 4)
        def _(part):
            lines = pl.ds(part * 4, 4)
            block = lax.dot_general(
                up[lines].reshape(4 * cols, channels),
                wbuf[...],
                (((1,), (1,)), ((), ())),
                preferred_element_type=jnp.float32,
            )
            bm[lines] = block.astype(jnp.bfloat16).reshape(4, cols, channels)

        save_mixed = pltpu.make_async_copy(bm.at[pl.ds(2, rows)], mixed.at[replica, micro], sems.at[1])
        save_mixed.start()
        column = lax.broadcasted_iota(jnp.int32, (cols, LANES), 0)

        @pl.loop(0, channels // LANES)
        def _(block):
            lanes = lane_block(block)

            @pl.loop(0, rows)
            def _(row):
                out[row, :, lanes] = row_conv(bm, row, lanes, taps, cols, column, -1).astype(jnp.bfloat16)

        stores = [
            pltpu.make_async_copy(out, sent, sems.at[2]),
            pltpu.make_async_copy(out.at[pl.ds(0, 2)], sent_top, sems.at[3]),
            pltpu.make_async_copy(out.at[pl.ds(rows - 2, 2)], sent_bot, sems.at[4]),
            pltpu.make_async_copy(out, outs.at[replica, micro], sems.at[5]),
        ]
        for store in stores:
            store.start()
        save_gates.wait()
        save_mixed.wait()
        for store in stores:
            store.wait()


def chain_step(replica, meta, recv, entry, masks, weight, kern, buffers):
    _, _, _, _, _, rows, cols, channels = masks[0].shape
    micro = masks[0].shape[3]
    fresh = buffers is None
    strip = jax.ShapeDtypeStruct((rows, cols, channels), jnp.bfloat16)
    edge = jax.ShapeDtypeStruct((2, cols, channels), jnp.bfloat16)
    whole = jax.ShapeDtypeStruct((2, micro, rows, cols, channels), jnp.bfloat16)
    operands = [meta, *recv, *entry, *masks, weight, kern]
    if not fresh:
        operands += list(buffers)
    results = pl.pallas_call(
        functools.partial(chain_kernel, replica, rows, cols, fresh),
        out_shape=(strip, edge, edge, whole, whole, whole),
        in_specs=[SMEM] + [ANY] * (len(operands) - 1),
        out_specs=(ANY,) * 6,
        scratch_shapes=[
            pltpu.VMEM((rows + 4, cols, channels), jnp.bfloat16),
            pltpu.VMEM((rows, cols, channels), jnp.int32),
            pltpu.VMEM((4, cols, channels), jnp.bfloat16),
            pltpu.VMEM((channels, channels), jnp.bfloat16),
            pltpu.VMEM((25, channels), jnp.float32),
            pltpu.VMEM((25, TILE, channels), CT),
            pltpu.VMEM((rows + 4, cols, channels), jnp.bfloat16),
            pltpu.VMEM((rows, cols, channels), jnp.bfloat16),
            pltpu.SemaphoreType.DMA((8,)),
        ],
        input_output_aliases={} if fresh else {12: 3, 13: 4, 14: 5},
        compiler_params=pltpu.CompilerParams(vmem_limit_bytes=40 << 20),
        cost_estimate=pl.CostEstimate(flops=60 * rows * cols * channels * 10, bytes_accessed=16 << 20, transcendentals=0),
    )(*operands)
    return results[:3], results[3:]


def grads_kernel(rows, cols, meta, acts, act_top, act_bot, kern, _mixed, _gates, wgrad, kgrad, mixed, gates, framed, kbuf, taps, bm, gated, depth, wsum, ksum, kout, sems):
    channels = framed.shape[2]
    replica = meta[0]
    micro = meta[1]
    loads = [
        pltpu.make_async_copy(acts.at[replica, 0, 0, micro, 0], framed.at[pl.ds(2, rows)], sems.at[0]),
        pltpu.make_async_copy(act_top.at[replica, micro], framed.at[pl.ds(0, 2)], sems.at[1]),
        pltpu.make_async_copy(act_bot.at[replica, micro], framed.at[pl.ds(rows + 2, 2)], sems.at[2]),
        pltpu.make_async_copy(kern.at[replica], kbuf, sems.at[3]),
        pltpu.make_async_copy(mixed.at[replica, micro], bm, sems.at[4]),
        pltpu.make_async_copy(gates.at[replica, micro], gated, sems.at[5]),
    ]
    for load in loads:
        load.start()
    for load in loads:
        load.wait()
    spread_kernel(kbuf, taps)
    column = lax.broadcasted_iota(jnp.int32, (cols, LANES), 0)
    ksum[...] = jnp.zeros_like(ksum)

    @pl.loop(0, channels // LANES)
    def _(block):
        lanes = lane_block(block)

        @pl.loop(0, rows)
        def _(row):
            depth[row, :, lanes] = row_conv(framed, row, lanes, taps, cols, column, 1).astype(jnp.bfloat16)

        @pl.loop(0, rows)
        def _(row):
            wide = bm[row, :, lanes].astype(jnp.float32)
            for col_tap in range(5):
                moved = shifted(wide, 2 - col_tap, column).astype(CT).reshape(cols // TILE, TILE, LANES)
                for row_tap in range(5):
                    line = framed[row + row_tap, :, lanes].astype(CT).reshape(cols // TILE, TILE, LANES)
                    part = moved * line
                    short = part[0]
                    for piece in range(1, cols // TILE):
                        short = short + part[piece]
                    short = short.astype(jnp.float32).reshape(TILE // 8, 8, LANES)
                    tap = row_tap * 5 + col_tap
                    ksum[tap, :, lanes] = ksum[tap, :, lanes] + jnp.sum(short, axis=0)

    wsum[...] = jnp.zeros_like(wsum)

    @pl.loop(0, rows // 8)
    def _(part):
        lines = pl.ds(part * 8, 8)
        wsum[...] += lax.dot_general(
            depth[lines].reshape(8 * cols, channels),
            gated[lines].reshape(8 * cols, channels),
            (((0,), (0,)), ((), ())),
            preferred_element_type=jnp.float32,
        )

    kout[...] = jnp.sum(ksum[...], axis=1)
    stores = [
        pltpu.make_async_copy(wsum, wgrad, sems.at[0]),
        pltpu.make_async_copy(kout, kgrad, sems.at[1]),
    ]
    for store in stores:
        store.start()
    for store in stores:
        store.wait()


def grads_step(meta, acts, kern, mixed, gates):
    _, _, _, micro, _, rows, cols, channels = acts[0].shape
    strip = pltpu.VMEM((rows, cols, channels), jnp.bfloat16)
    whole = jax.ShapeDtypeStruct((2, micro, rows, cols, channels), jnp.bfloat16)
    return pl.pallas_call(
        functools.partial(grads_kernel, rows, cols),
        out_shape=(
            jax.ShapeDtypeStruct((channels, channels), jnp.float32),
            jax.ShapeDtypeStruct((25, channels), jnp.float32),
            whole,
            whole,
        ),
        in_specs=[SMEM] + [ANY] * 6,
        out_specs=(ANY,) * 4,
        scratch_shapes=[
            pltpu.VMEM((rows + 4, cols, channels), jnp.bfloat16),
            pltpu.VMEM((25, channels), jnp.float32),
            pltpu.VMEM((25, TILE, channels), CT),
            strip,
            strip,
            strip,
            pltpu.VMEM((channels, channels), jnp.float32),
            pltpu.VMEM((25, 8, channels), jnp.float32),
            pltpu.VMEM((25, channels), jnp.float32),
            pltpu.SemaphoreType.DMA((6,)),
        ],
        input_output_aliases={5: 2, 6: 3},
        compiler_params=pltpu.CompilerParams(vmem_limit_bytes=40 << 20),
        cost_estimate=pl.CostEstimate(flops=120 * rows * cols * channels * 10, bytes_accessed=8 << 20, transcendentals=0),
    )(meta, *acts, kern, mixed, gates)


def edges(cells, dim):
    count = lax.axis_size("strip")
    size = cells.shape[dim]
    head = lax.slice_in_dim(cells, 0, 2, axis=dim)
    tail = lax.slice_in_dim(cells, size - 2, size, axis=dim)
    above = lax.ppermute(tail, "strip", [(i, i + 1) for i in range(count - 1)])
    below = lax.ppermute(head, "strip", [(i + 1, i) for i in range(count - 1)])
    return above, below


def passed_along(values, by, sources):
    main, head, tail = values
    count = lax.axis_size("strip")
    axes = ("sec", "strip")
    above = lax.ppermute(
        tail, axes, [(p * count + z, (p + by) * count + z + 1) for p in sources for z in range(count - 1)]
    )
    below = lax.ppermute(
        head, axes, [(p * count + z + 1, (p + by) * count + z) for p in sources for z in range(count - 1)]
    )
    main = lax.ppermute(main, "sec", [(p, p + by) for p in sources])
    return main, above, below


def timetable(sections, micro):
    order = []
    for p in range(sections):
        runs = [(m + sections - 1 - p, 0, m) for m in range(micro)] + [(m + p, 1, m) for m in range(micro)]
        order.append(sorted(runs))
    ready = [max(order[p][k][0] for p in range(sections)) for k in range(2 * micro)]
    table = np.array([[run[1:] for run in runs] for runs in order], np.int32)
    return table, ready


def body(activations, relu_masks, grad_in, mix_weight, depth_kernel):
    sections = lax.axis_size("sec")
    position = lax.axis_index("sec")
    micro = activations.shape[3]
    rows, cols, channels = activations.shape[5:]
    mirror = [(i, sections - 1 - i) for i in range(sections)]

    mask_ends = jnp.concatenate([relu_masks[:, 0, 0, :, 0, :2], relu_masks[:, 0, 0, :, 0, -2:]], axis=2)
    mask_ends = (mask_ends == 1).astype(jnp.bfloat16)
    grad_ends = jnp.concatenate([grad_in[:, :, 0, :2], grad_in[:, :, 0, -2:]], axis=2)
    first = edges(jnp.stack([mask_ends, grad_ends]), 3)
    mask_top, grad_top = first[0][0], first[0][1]
    mask_bot, grad_bot = first[1][0], first[1][1]
    packed = jnp.concatenate([mix_weight[0, 0], depth_kernel[0, 0]], axis=0)
    mirrored = lax.ppermute(packed, "sec", mirror)
    weights = jnp.stack([mix_weight[0, 0], mirrored[:channels]])
    kernels = jnp.stack([depth_kernel[0, 0], mirrored[channels:]]).astype(jnp.float32)
    act_top, act_bot = edges(activations[:, 0, 0, :, 0], 2)

    masks = (relu_masks, mask_top, mask_bot)
    entry = (grad_in, grad_top, grad_bot)
    acts = (activations, act_top, act_bot)
    table, ready = timetable(sections, micro)
    table = jnp.asarray(table)[position]

    edge = jnp.zeros((2, cols, channels), jnp.bfloat16)
    nothing = (jnp.zeros((rows, cols, channels), jnp.bfloat16), edge, edge)
    received = [nothing, nothing]
    buffers = None
    grads_w = [0.0, 0.0]
    grads_k = [0.0, 0.0]
    ticks = micro + sections - 1
    for tick in range(ticks):
        waiting = received
        received = [None, None]
        for replica in range(2):
            depth_in = sections - 1 - position if replica == 0 else position
            wanted = tick - depth_in
            valid = (wanted >= 0) & (wanted < micro)
            meta = jnp.stack([valid, jnp.clip(wanted, 0, micro - 1), depth_in == 0]).astype(jnp.int32)
            values, buffers = chain_step(
                replica, meta, waiting[replica], entry, masks, weights, kernels, buffers
            )
            if tick < ticks - 1:
                by = -1 if replica == 0 else 1
                sources = [
                    p
                    for p in range(sections)
                    if 0 <= p + by < sections
                    and 0 <= tick - (sections - 1 - p if replica == 0 else p) < micro
                ]
                received[replica] = passed_along(values, by, sources)
        for k in range(2 * micro):
            if ready[k] != tick:
                continue
            run = table[k]
            outs, mixed, gates = buffers
            wgrad, kgrad, mixed, gates = grads_step(run, acts, kernels, mixed, gates)
            buffers = (outs, mixed, gates)
            for replica in range(2):
                mine = run[0] == replica
                grads_w[replica] = grads_w[replica] + jnp.where(mine, wgrad, 0.0)
                grads_k[replica] = grads_k[replica] + jnp.where(mine, kgrad, 0.0)

    factor = 1.0 / H
    both_w = jnp.concatenate(grads_w, axis=1).astype(jnp.bfloat16)
    shares = lax.psum_scatter(both_w, "strip", scatter_dimension=0, tiled=True).astype(jnp.float32)
    kernel_all = lax.psum(jnp.stack(grads_k).astype(jnp.bfloat16), "strip").astype(jnp.float32)
    share_rows = shares.shape[0]
    partner = jnp.concatenate([shares[:, channels:], kernel_all[1]], axis=0).astype(jnp.bfloat16)
    partner = lax.ppermute(partner, "sec", mirror).astype(jnp.float32)
    share_w = (shares[:, :channels] + partner[:share_rows]) * factor
    full_k = (kernel_all[0] + partner[share_rows:]) * factor
    return buffers[0][:, None, :, None], share_w[None, None], full_k[None, None]


def solution(mesh):
    placed = (
        P(None, "sec", None, None, None, "strip", None, None),
        P(None, "sec", None, None, None, "strip", None, None),
        P(None, None, None, "strip", None, None),
        P("sec", None, None, None),
        P("sec", None, None, None),
    )
    return jax.shard_map(
        body,
        mesh=mesh,
        in_specs=placed,
        out_specs=(
            P(None, "sec", None, None, "strip", None, None),
            P("sec", None, "strip", None),
            P("sec", None, None, None),
        ),
        check_vma=False,
    )
```

```python
import functools

import jax
import jax.numpy as jnp
import numpy as np
from jax import lax
from jax.experimental import pallas as pl
from jax.experimental.pallas import tpu as pltpu
from jax.sharding import PartitionSpec as P

H = 256
LANES = 128
CT = jnp.bfloat16
TILE = 16
ANY = pl.BlockSpec(memory_space=pltpu.HBM)
SMEM = pl.BlockSpec(memory_space=pltpu.SMEM)


def lane_block(block):
    return pl.ds(pl.multiple_of(block * LANES, LANES), LANES)


def shifted(value, offset, column):
    if offset == 0:
        return value
    cols = value.shape[0]
    turned = pltpu.roll(value, (-offset) % cols, 0)
    inside = column < cols - offset if offset > 0 else column >= -offset
    return jnp.where(inside, turned, 0.0)


def row_conv(source, row, lanes, taps, cols, column, sign):
    total = [None] * 5
    for row_tap in range(5):
        place = row + (row_tap if sign == 1 else 4 - row_tap)
        line = source[place, :, lanes].astype(CT).reshape(cols // TILE, TILE, LANES)
        for col_tap in range(5):
            term = line * taps[row_tap * 5 + col_tap, :, lanes][None]
            total[col_tap] = term if total[col_tap] is None else total[col_tap] + term
    out = None
    for col_tap in range(5):
        part = total[col_tap].reshape(cols, LANES).astype(jnp.float32)
        part = shifted(part, sign * (col_tap - 2), column)
        out = part if out is None else out + part
    return out


def spread_kernel(kern_ref, taps):
    channels = kern_ref.shape[1]
    for tap in range(25):
        taps[tap] = jnp.broadcast_to(kern_ref[tap : tap + 1, :].astype(CT), (TILE, channels))


def chain_kernel(replica, rows, cols, fresh, *refs):
    meta, recv, recv_top, recv_bot, entry, entry_top, entry_bot, masks, mask_top, mask_bot, weight, kern = refs[:12]
    refs = refs[12 if fresh else 15 :]
    sent, outs, mixed, gates = refs[:4]
    up, seen, seen_halo, wbuf, kbuf, taps, bm, out, sems = refs[4:]
    channels = up.shape[2]
    micro = meta[1]

    @pl.when(meta[0] == 1)
    def _():
        loads = [
            pltpu.make_async_copy(masks.at[replica, 0, 0, micro, 0], seen, sems.at[0]),
            pltpu.make_async_copy(mask_top.at[replica, micro], seen_halo.at[pl.ds(0, 2)], sems.at[1]),
            pltpu.make_async_copy(mask_bot.at[replica, micro], seen_halo.at[pl.ds(2, 2)], sems.at[2]),
            pltpu.make_async_copy(weight.at[replica], wbuf, sems.at[3]),
            pltpu.make_async_copy(kern.at[replica], kbuf, sems.at[4]),
        ]
        for load in loads:
            load.start()

        def fetch(main, top, bot):
            pieces = [
                pltpu.make_async_copy(main, up.at[pl.ds(2, rows)], sems.at[5]),
                pltpu.make_async_copy(top, up.at[pl.ds(0, 2)], sems.at[6]),
                pltpu.make_async_copy(bot, up.at[pl.ds(rows + 2, 2)], sems.at[7]),
            ]
            for piece in pieces:
                piece.start()
            for piece in pieces:
                piece.wait()

        @pl.when(meta[2] == 1)
        def _():
            fetch(entry.at[replica, micro, 0], entry_top.at[replica, micro], entry_bot.at[replica, micro])

        @pl.when(meta[2] == 0)
        def _():
            fetch(recv, recv_top, recv_bot)

        for load in loads:
            load.wait()
        spread_kernel(kbuf, taps)
        for line in range(2):
            up[line] = up[line] * seen_halo[line]
            up[rows + 2 + line] = up[rows + 2 + line] * seen_halo[2 + line]

        @pl.loop(0, rows)
        def _(row):
            value = up[row + 2].astype(jnp.float32)
            up[row + 2] = jnp.where(seen[row] == 1, value, 0.0).astype(jnp.bfloat16)

        save_gates = pltpu.make_async_copy(up.at[pl.ds(2, rows)], gates.at[replica, micro], sems.at[0])
        save_gates.start()

        @pl.loop(0, (rows + 4) // 4)
        def _(part):
            lines = pl.ds(part * 4, 4)
            block = lax.dot_general(
                up[lines].reshape(4 * cols, channels),
                wbuf[...],
                (((1,), (1,)), ((), ())),
                preferred_element_type=jnp.float32,
            )
            bm[lines] = block.astype(jnp.bfloat16).reshape(4, cols, channels)

        save_mixed = pltpu.make_async_copy(bm.at[pl.ds(2, rows)], mixed.at[replica, micro], sems.at[1])
        save_mixed.start()
        column = lax.broadcasted_iota(jnp.int32, (cols, LANES), 0)

        @pl.loop(0, channels // LANES)
        def _(block):
            lanes = lane_block(block)

            @pl.loop(0, rows)
            def _(row):
                out[row, :, lanes] = row_conv(bm, row, lanes, taps, cols, column, -1).astype(jnp.bfloat16)

        stores = [
            pltpu.make_async_copy(out, sent, sems.at[2]),
            pltpu.make_async_copy(out, outs.at[replica, micro], sems.at[5]),
        ]
        for store in stores:
            store.start()
        save_gates.wait()
        save_mixed.wait()
        for store in stores:
            store.wait()


def chain_step(replica, meta, recv, entry, masks, weight, kern, buffers):
    _, _, _, _, _, rows, cols, channels = masks[0].shape
    micro = masks[0].shape[3]
    fresh = buffers is None
    strip = jax.ShapeDtypeStruct((rows, cols, channels), jnp.bfloat16)
    whole = jax.ShapeDtypeStruct((2, micro, rows, cols, channels), jnp.bfloat16)
    operands = [meta, *recv, *entry, *masks, weight, kern]
    if not fresh:
        operands += list(buffers)
    results = pl.pallas_call(
        functools.partial(chain_kernel, replica, rows, cols, fresh),
        out_shape=(strip, whole, whole, whole),
        in_specs=[SMEM] + [ANY] * (len(operands) - 1),
        out_specs=(ANY,) * 4,
        scratch_shapes=[
            pltpu.VMEM((rows + 4, cols, channels), jnp.bfloat16),
            pltpu.VMEM((rows, cols, channels), jnp.int32),
            pltpu.VMEM((4, cols, channels), jnp.bfloat16),
            pltpu.VMEM((channels, channels), jnp.bfloat16),
            pltpu.VMEM((25, channels), jnp.float32),
            pltpu.VMEM((25, TILE, channels), CT),
            pltpu.VMEM((rows + 4, cols, channels), jnp.bfloat16),
            pltpu.VMEM((rows, cols, channels), jnp.bfloat16),
            pltpu.SemaphoreType.DMA((8,)),
        ],
        input_output_aliases={} if fresh else {12: 1, 13: 2, 14: 3},
        compiler_params=pltpu.CompilerParams(vmem_limit_bytes=60 << 20),
        cost_estimate=pl.CostEstimate(flops=60 * rows * cols * channels * 10, bytes_accessed=16 << 20, transcendentals=0),
    )(*operands)
    return results[0], results[1:]


def depth_kernel_body(rows, cols, meta, acts, act_top, act_bot, kern, _mixed, result, mixed, framed, kbuf, taps, depth, sems):
    channels = framed.shape[2]
    replica = meta[0]
    micro = meta[1]
    loads = [
        pltpu.make_async_copy(acts.at[replica, 0, 0, micro, 0], framed.at[pl.ds(2, rows)], sems.at[0]),
        pltpu.make_async_copy(act_top.at[replica, micro], framed.at[pl.ds(0, 2)], sems.at[1]),
        pltpu.make_async_copy(act_bot.at[replica, micro], framed.at[pl.ds(rows + 2, 2)], sems.at[2]),
        pltpu.make_async_copy(kern.at[replica], kbuf, sems.at[3]),
    ]
    for load in loads:
        load.start()
    for load in loads:
        load.wait()
    spread_kernel(kbuf, taps)
    column = lax.broadcasted_iota(jnp.int32, (cols, LANES), 0)

    @pl.loop(0, channels // LANES)
    def _(block):
        lanes = lane_block(block)

        @pl.loop(0, rows)
        def _(row):
            depth[row, :, lanes] = row_conv(framed, row, lanes, taps, cols, column, 1).astype(jnp.bfloat16)

    store = pltpu.make_async_copy(depth, result, sems.at[0])
    store.start()
    store.wait()


def depth_step(meta, acts, kern, mixed):
    _, _, _, micro, _, rows, cols, channels = acts[0].shape
    return pl.pallas_call(
        functools.partial(depth_kernel_body, rows, cols),
        out_shape=(
            jax.ShapeDtypeStruct((rows, cols, channels), jnp.bfloat16),
            jax.ShapeDtypeStruct(mixed.shape, mixed.dtype),
        ),
        in_specs=[SMEM] + [ANY] * 5,
        out_specs=(ANY,) * 2,
        scratch_shapes=[
            pltpu.VMEM((rows + 4, cols, channels), jnp.bfloat16),
            pltpu.VMEM((25, channels), jnp.float32),
            pltpu.VMEM((25, TILE, channels), CT),
            pltpu.VMEM((rows, cols, channels), jnp.bfloat16),
            pltpu.SemaphoreType.DMA((4,)),
        ],
        input_output_aliases={5: 1},
        compiler_params=pltpu.CompilerParams(vmem_limit_bytes=60 << 20),
        cost_estimate=pl.CostEstimate(flops=60 * rows * cols * channels * 10, bytes_accessed=4 << 20, transcendentals=0),
    )(meta, *acts, kern, mixed)


def grads_kernel(rows, cols, given, *refs):
    meta, acts, act_top, act_bot, kern = refs[:5]
    ready_depth = refs[7] if given else None
    refs = refs[8 if given else 7 :]
    wgrad, kgrad, mixed, gates, framed, kbuf, taps, bm, gated, depth, wsum, ksum, kout, sems = refs
    channels = framed.shape[2]
    replica = meta[0]
    micro = meta[1]
    loads = [
        pltpu.make_async_copy(acts.at[replica, 0, 0, micro, 0], framed.at[pl.ds(2, rows)], sems.at[0]),
        pltpu.make_async_copy(act_top.at[replica, micro], framed.at[pl.ds(0, 2)], sems.at[1]),
        pltpu.make_async_copy(act_bot.at[replica, micro], framed.at[pl.ds(rows + 2, 2)], sems.at[2]),
        pltpu.make_async_copy(kern.at[replica], kbuf, sems.at[3]),
        pltpu.make_async_copy(mixed.at[replica, micro], bm, sems.at[4]),
        pltpu.make_async_copy(gates.at[replica, micro], gated, sems.at[5]),
    ]
    if given:
        loads.append(pltpu.make_async_copy(ready_depth, depth, sems.at[6]))
    for load in loads:
        load.start()
    for load in loads:
        load.wait()
    spread_kernel(kbuf, taps)
    column = lax.broadcasted_iota(jnp.int32, (cols, LANES), 0)
    ksum[...] = jnp.zeros_like(ksum)

    @pl.loop(0, channels // LANES)
    def _(block):
        lanes = lane_block(block)

        if not given:
            @pl.loop(0, rows)
            def _(row):
                depth[row, :, lanes] = row_conv(framed, row, lanes, taps, cols, column, 1).astype(jnp.bfloat16)

        @pl.loop(0, rows)
        def _(row):
            wide = bm[row, :, lanes].astype(jnp.float32)
            for col_tap in range(5):
                moved = shifted(wide, 2 - col_tap, column).astype(CT).reshape(cols // TILE, TILE, LANES)
                for row_tap in range(5):
                    line = framed[row + row_tap, :, lanes].astype(CT).reshape(cols // TILE, TILE, LANES)
                    part = moved * line
                    short = part[0]
                    for piece in range(1, cols // TILE):
                        short = short + part[piece]
                    short = short.astype(jnp.float32).reshape(TILE // 8, 8, LANES)
                    tap = row_tap * 5 + col_tap
                    ksum[tap, :, lanes] = ksum[tap, :, lanes] + jnp.sum(short, axis=0)

    wsum[...] = jnp.zeros_like(wsum)

    @pl.loop(0, rows // 8)
    def _(part):
        lines = pl.ds(part * 8, 8)
        wsum[...] += lax.dot_general(
            depth[lines].reshape(8 * cols, channels),
            gated[lines].reshape(8 * cols, channels),
            (((0,), (0,)), ((), ())),
            preferred_element_type=jnp.float32,
        )

    kout[...] = jnp.sum(ksum[...], axis=1)
    stores = [
        pltpu.make_async_copy(wsum, wgrad, sems.at[0]),
        pltpu.make_async_copy(kout, kgrad, sems.at[1]),
    ]
    for store in stores:
        store.start()
    for store in stores:
        store.wait()


def grads_step(meta, acts, kern, mixed, gates, depth):
    _, _, _, micro, _, rows, cols, channels = acts[0].shape
    strip = pltpu.VMEM((rows, cols, channels), jnp.bfloat16)
    whole = jax.ShapeDtypeStruct((2, micro, rows, cols, channels), jnp.bfloat16)
    return pl.pallas_call(
        functools.partial(grads_kernel, rows, cols, depth is not None),
        out_shape=(
            jax.ShapeDtypeStruct((channels, channels), jnp.float32),
            jax.ShapeDtypeStruct((25, channels), jnp.float32),
            whole,
            whole,
        ),
        in_specs=[SMEM] + [ANY] * (6 if depth is None else 7),
        out_specs=(ANY,) * 4,
        scratch_shapes=[
            pltpu.VMEM((rows + 4, cols, channels), jnp.bfloat16),
            pltpu.VMEM((25, channels), jnp.float32),
            pltpu.VMEM((25, TILE, channels), CT),
            strip,
            strip,
            strip,
            pltpu.VMEM((channels, channels), jnp.float32),
            pltpu.VMEM((25, 8, channels), jnp.float32),
            pltpu.VMEM((25, channels), jnp.float32),
            pltpu.SemaphoreType.DMA((7,)),
        ],
        input_output_aliases={5: 2, 6: 3},
        compiler_params=pltpu.CompilerParams(vmem_limit_bytes=60 << 20),
        cost_estimate=pl.CostEstimate(flops=120 * rows * cols * channels * 10, bytes_accessed=8 << 20, transcendentals=0),
    )(meta, *acts, kern, mixed, gates, *([] if depth is None else [depth]))


def edges(cells, dim):
    count = lax.axis_size("strip")
    size = cells.shape[dim]
    head = lax.slice_in_dim(cells, 0, 2, axis=dim)
    tail = lax.slice_in_dim(cells, size - 2, size, axis=dim)
    above = lax.ppermute(tail, "strip", [(i, i + 1) for i in range(count - 1)])
    below = lax.ppermute(head, "strip", [(i + 1, i) for i in range(count - 1)])
    return above, below


def passed_along(main, by, sources):
    return lax.ppermute(main, "sec", [(p, p + by) for p in sources])


def strip_sums(wide, taps):
    count = lax.axis_size("strip")
    place = lax.axis_index("strip")
    steps = count.bit_length() - 1
    share = wide.shape[0] // count
    columns = wide.shape[1]
    blocks = wide.reshape(count, share, columns)
    for step in range(steps):
        side = (place >> step) & 1
        pairs = blocks.reshape(-1, 2, share, columns)
        kept = lax.dynamic_index_in_dim(pairs, side, 1, keepdims=False)
        given = lax.dynamic_index_in_dim(pairs, 1 - side, 1, keepdims=False)
        sent = jnp.concatenate([given.reshape(-1, columns), taps]).astype(jnp.bfloat16)
        got = lax.ppermute(sent, "strip", [(i, i ^ (1 << step)) for i in range(count)]).astype(jnp.float32)
        rows = got.shape[0] - taps.shape[0]
        blocks = kept + got[:rows].reshape(kept.shape)
        taps = taps + got[rows:]
    return blocks.reshape(share, columns), taps


def timetable(sections, micro):
    order = []
    for p in range(sections):
        runs = [(m + sections - 1 - p, 0, m) for m in range(micro)] + [(m + p, 1, m) for m in range(micro)]
        order.append(sorted(runs))
    ready = [max(order[p][k][0] for p in range(sections)) for k in range(2 * micro)]
    table = np.array([[run[1:] for run in runs] for runs in order], np.int32)
    return table, ready


def body(activations, relu_masks, grad_in, mix_weight, depth_kernel):
    sections = lax.axis_size("sec")
    position = lax.axis_index("sec")
    micro = activations.shape[3]
    rows, cols, channels = activations.shape[5:]
    mirror = [(i, sections - 1 - i) for i in range(sections)]

    mask_ends = jnp.concatenate([relu_masks[:, 0, 0, :, 0, :2], relu_masks[:, 0, 0, :, 0, -2:]], axis=2)
    mask_ends = (mask_ends == 1).astype(jnp.bfloat16)
    grad_ends = jnp.concatenate([grad_in[:, :, 0, :2], grad_in[:, :, 0, -2:]], axis=2)
    first = edges(jnp.stack([mask_ends, grad_ends]), 3)
    mask_top, grad_top = first[0][0], first[0][1]
    mask_bot, grad_bot = first[1][0], first[1][1]
    packed = jnp.concatenate([mix_weight[0, 0], depth_kernel[0, 0]], axis=0)
    mirrored = lax.ppermute(packed, "sec", mirror)
    weights = jnp.stack([mix_weight[0, 0], mirrored[:channels]])
    kernels = jnp.stack([depth_kernel[0, 0], mirrored[channels:]]).astype(jnp.float32)
    act_top, act_bot = edges(activations[:, 0, 0, :, 0], 2)

    masks = (relu_masks, mask_top, mask_bot)
    entry = (grad_in, grad_top, grad_bot)
    acts = (activations, act_top, act_bot)
    table, ready = timetable(sections, micro)
    table = jnp.asarray(table)[position]

    edge = jnp.zeros((2, cols, channels), jnp.bfloat16)
    nothing = (jnp.zeros((rows, cols, channels), jnp.bfloat16), edge, edge)
    received = [nothing, nothing]
    buffers = None
    grads_w = [0.0, 0.0]
    grads_k = [0.0, 0.0]
    ticks = micro + sections - 1
    for tick in range(ticks):
        waiting = received
        received = [None, None]
        for replica in range(2):
            depth_in = sections - 1 - position if replica == 0 else position
            wanted = tick - depth_in
            valid = (wanted >= 0) & (wanted < micro)
            meta = jnp.stack([valid, jnp.clip(wanted, 0, micro - 1), depth_in == 0]).astype(jnp.int32)
            values, buffers = chain_step(
                replica, meta, waiting[replica], entry, masks, weights, kernels, buffers
            )
            if tick < ticks - 1:
                by = -1 if replica == 0 else 1
                sources = [
                    p
                    for p in range(sections)
                    if 0 <= p + by < sections
                    and 0 <= tick - (sections - 1 - p if replica == 0 else p) < micro
                ]
                received[replica] = passed_along(values, by, sources)
        if tick == 0:
            outs, mixed, gates = buffers
            early, mixed = depth_step(table[2 * micro - 1], acts, kernels, mixed)
            latest = early
            buffers = (outs, mixed, gates)
        for k in range(2 * micro):
            if ready[k] != tick:
                continue
            run = table[k]
            outs, mixed, gates = buffers
            given = early if k == 2 * micro - 1 else None
            wgrad, kgrad, mixed, gates = grads_step(run, acts, kernels, mixed, gates, given)
            latest = kgrad
            buffers = (outs, mixed, gates)
            for replica in range(2):
                mine = run[0] == replica
                grads_w[replica] = grads_w[replica] + jnp.where(mine, wgrad, 0.0)
                grads_k[replica] = grads_k[replica] + jnp.where(mine, kgrad, 0.0)

        if tick < ticks - 1:
            for replica in range(2):
                main, _ = lax.optimization_barrier((received[replica], latest))
                received[replica] = (main, *edges(main, 0))

    factor = 1.0 / H
    shares, kernel_all = strip_sums(jnp.concatenate(grads_w, axis=1), jnp.concatenate(grads_k, axis=1))
    share_rows = shares.shape[0]
    partner = jnp.concatenate([shares[:, channels:], kernel_all[:, channels:]], axis=0).astype(jnp.bfloat16)
    partner = lax.ppermute(partner, "sec", mirror).astype(jnp.float32)
    share_w = (shares[:, :channels] + partner[:share_rows]) * factor
    full_k = (kernel_all[:, :channels] + partner[share_rows:]) * factor
    return buffers[0][:, None, :, None], share_w[None, None], full_k[None, None]


def solution(mesh):
    placed = (
        P(None, "sec", None, None, None, "strip", None, None),
        P(None, "sec", None, None, None, "strip", None, None),
        P(None, None, None, "strip", None, None),
        P("sec", None, None, None),
        P("sec", None, None, None),
    )
    return jax.shard_map(
        body,
        mesh=mesh,
        in_specs=placed,
        out_specs=(
            P(None, "sec", None, None, "strip", None, None),
            P("sec", None, "strip", None),
            P("sec", None, None, None),
        ),
        check_vma=False,
    )
```
